32 devices in a mesh: leaf: 2 (over y), row: 4 (over x, core), col: 4 (over z).
Axes of the slice: x: 2, y: 2, z: 4, core: 2. Of those that a mesh axis runs over, the one named last changes fastest.
Arguments:
- parent_entries: float32 [8, 8, 256, 16, 4, 256], P(None, ('leaf', 'row'), None, None, 'col'), may hold values from -1 to 32, as said below
- block_pattern: int32 [64, 64], replicated, may hold values 0 or 1
- child_map: int32 [2, 32], replicated, may hold values from 0 to 63, as said below
- child_schur: float32 [2, 8, 4, 256, 8, 4, 256], P('leaf', None, 'row', None, None, 'col'), may hold values from -1 to 1
Outputs:
- factored_front: float32 [8, 8, 256, 16, 4, 256], P(None, ('leaf', 'row'), None, None, 'col')
The draws below stay inside these ranges and needn't reach their ends.
Inputs may be any that keep to these rules, and one draw needn't show every extreme that they name: For each child the 32 entries are distinct, and child_map[l, a] - a is a multiple of 4. `parent_entries`: the leading 2 * 512 rows and columns of front, as the symmetric matrix of its lower triangle, are positive definite.
All inputs are finite; a program needn't handle non-finite values.
Results may differ from the reference program's by a relative error of at most 0.0001.
Values sent between devices are 32-bit elements; how exact they have to be, the bound alone decides.
No kernel may reach another device: no remote copies, remote signals or barrier semaphores. Data moves between devices by JAX's collectives and lax.ppermute only.
A program may use at most 320 MiB of HBM per device.

```python
import math
import jax
import jax.numpy as jnp
from jax import lax

BLOCK_EDGE = 256
PB = 2
NPANEL = 2
FB = 64
CB = 32
PW = 512
CHILD_GRID_ROWS = 4
GRID_COLUMNS = 4
CHILD_COUNT = 2
PR = 8
LR = 8
LC = 16
CHILD_BLOCK_ROWS = 8
CHILD_BLOCK_COLS = 8


def block_targets(key):
    per_residue = CB // GRID_COLUMNS
    level_count = FB // GRID_COLUMNS
    keys = jax.random.split(key, CHILD_COUNT * GRID_COLUMNS)

    def one_residue(sub_key):
        inner = jax.random.permutation(sub_key, level_count - 2) + 1
        picked = jnp.concatenate([jnp.array([0, level_count - 1], dtype=jnp.int32), inner[:per_residue - 2].astype(jnp.int32)])
        return jnp.sort(picked)
    levels = jax.vmap(one_residue)(keys).reshape(CHILD_COUNT, GRID_COLUMNS, per_residue)
    residues = jnp.arange(GRID_COLUMNS, dtype=jnp.int32)[None, :, None]
    mapped = levels * GRID_COLUMNS + residues
    return jnp.transpose(mapped, (0, 2, 1)).reshape(CHILD_COUNT, CB)


def lead_scale():
    return 3.2 / math.sqrt(NPANEL * PW)


def draw_child_map(key, part):
    return block_targets(jax.random.fold_in(key, 17))


def draw_child_schur(key, part):
    targets = block_targets(jax.random.fold_in(key, 17))
    in_lead = jnp.repeat(targets < NPANEL * PB, BLOCK_EDGE, axis=1)
    entry_values = jax.random.uniform(jax.random.fold_in(key, 29), (CHILD_COUNT, CB * BLOCK_EDGE, CB * BLOCK_EDGE), jnp.float32, -1.0, 1.0)
    both_lead = in_lead[:, :, None] & in_lead[:, None, :]
    either_lead = in_lead[:, :, None] | in_lead[:, None, :]
    scale_factor = jnp.where(both_lead, lead_scale(), jnp.where(either_lead, 0.5, 1.0))
    return (entry_values * scale_factor).reshape(CHILD_COUNT, CHILD_BLOCK_ROWS, CHILD_GRID_ROWS, BLOCK_EDGE, CHILD_BLOCK_COLS, GRID_COLUMNS, BLOCK_EDGE)


def draw_parent_entries(key, part):
    size = FB * BLOCK_EDGE
    positions = jnp.arange(size)
    in_lead = positions < NPANEL * PW
    entry_values = jax.random.uniform(jax.random.fold_in(key, 31), (size, size), jnp.float32, -1.0, 1.0)
    diagonal = jnp.exp(jax.random.uniform(jax.random.fold_in(key, 37), (size,), jnp.float32, math.log(16.0), math.log(32.0)))
    both_lead = in_lead[:, None] & in_lead[None, :]
    either_lead = in_lead[:, None] | in_lead[None, :]
    scale_factor = jnp.where(both_lead, lead_scale(), jnp.where(either_lead, 0.5, 1.0))
    result = entry_values * scale_factor
    on_diagonal = (positions[:, None] == positions[None, :]) & both_lead
    result = jnp.where(on_diagonal, diagonal[:, None], result)
    return result.reshape(LR, PR, BLOCK_EDGE, LC, GRID_COLUMNS, BLOCK_EDGE)


def with_ends(values, rng, least, largest):
    index_at = [jax.random.randint(jax.random.fold_in(rng, axis), (), 0, length) for axis, length in enumerate(values.shape)]
    widest = values.shape.index(max(values.shape))
    beside = index_at[:widest] + [(index_at[widest] + 1) % values.shape[widest]] + index_at[widest + 1:]
    return values.at[tuple(index_at)].set(least).at[tuple(beside)].set(largest)


def setup_inputs(seed: int = 0) -> dict:
    arg_keys = jax.random.split(jax.random.key(seed), 5)
    parent_entries = draw_parent_entries(jax.random.fold_in(arg_keys[4], 71), 0)
    block_pattern = with_ends((jax.random.randint(arg_keys[1], (FB, FB), 0, 2) < 1).astype(jnp.int32), jax.random.fold_in(arg_keys[1], 1), 0, 1)
    child_map = draw_child_map(jax.random.fold_in(arg_keys[4], 71), 0)
    child_schur = draw_child_schur(jax.random.fold_in(arg_keys[4], 71), 0)
    return {"parent_entries": parent_entries, "block_pattern": block_pattern, "child_map": child_map, "child_schur": child_schur}


def assemble(parent_entries, block_pattern, child_map, child_schur):
    blocks = parent_entries.reshape(FB, BLOCK_EDGE, FB, BLOCK_EDGE)
    kept_blocks = jnp.maximum(block_pattern, jnp.eye(FB, dtype=jnp.int32)).astype(jnp.float32)
    blocks = blocks * kept_blocks[:, None, :, None]
    for leaf_index in range(CHILD_COUNT):
        targets = child_map[leaf_index].astype(jnp.int32)
        pieces = child_schur[leaf_index].reshape(CB, BLOCK_EDGE, CB, BLOCK_EDGE)

        def add_row(which, current):
            target = lax.dynamic_index_in_dim(targets, which, 0, keepdims=False)
            piece = lax.dynamic_index_in_dim(pieces, which, 0, keepdims=False)
            row_block = lax.dynamic_index_in_dim(current, target, 0, keepdims=False)
            row_block = row_block.at[:, targets, :].add(piece)
            return lax.dynamic_update_index_in_dim(current, row_block, target, 0)
        blocks = lax.fori_loop(0, CB, add_row, blocks)
    return blocks.reshape(FB * BLOCK_EDGE, FB * BLOCK_EDGE)

def reference(parent_entries, block_pattern, child_map, child_schur):
    matrix = assemble(parent_entries, block_pattern, child_map, child_schur)
    for panel_index in range(NPANEL):
        first = panel_index * PW
        last = first + PW
        corner = matrix[first:last, first:last]
        symmetric = jnp.tril(corner) + jnp.tril(corner, -1).T
        factor = jnp.linalg.cholesky(symmetric)
        solved = lax.linalg.triangular_solve(factor, matrix[last:, first:last], left_side=False, lower=True, transpose_a=True)
        update = jnp.dot(solved.astype(jnp.float32), solved.T.astype(jnp.float32), precision=lax.Precision.HIGHEST, preferred_element_type=jnp.float32)
        matrix = matrix.at[last:, last:].add(-update)
        matrix = matrix.at[first:last, first:last].set(factor)
        matrix = matrix.at[last:, first:last].set(solved)
    return matrix.reshape(LR, PR, BLOCK_EDGE, LC, GRID_COLUMNS, BLOCK_EDGE)
```

```python
import functools

import jax
import jax.numpy as jnp
from jax import lax
from jax.experimental import pallas as pl
from jax.experimental.pallas import tpu as pltpu
from jax.sharding import PartitionSpec as P


PB = 2
NPANEL = 2
NB = PB * NPANEL
T = 128
STEP = 4
F32 = jnp.float32
BF16 = jnp.bfloat16
HIGH = lax.Precision.HIGHEST
NT = (((1,), (1,)), ((), ()))
NN = (((1,), (0,)), ((), ()))
MIB = 1 << 20


def split(value):
    high = value.astype(BF16)
    return high, (value - high.astype(F32)).astype(BF16)


def dot3(a_high, a_low, b_high, b_low, dims=NT):
    def one(a, b):
        return lax.dot_general(a, b, dims, preferred_element_type=F32)

    return one(a_high, b_high) + (one(a_high, b_low) + one(a_low, b_high))


def dot6(a, b, dims):
    return lax.dot_general(a, b, dims, precision=HIGH, preferred_element_type=F32)


def pack_kernel(width, order, spare, child, out):
    for slot in range(width - 1):
        source = slot + (slot >= spare[0]).astype(jnp.int32)
        for half in range(2):
            out[0, slot, :, half * T : half * T + T] = child[
                0, pl.ds(2 * source + half, out.shape[2], stride=2 * width), :
            ]


def pack(child, order, spare, slots, width):
    edge = child.shape[1] // (2 * width)
    return pl.pallas_call(
        functools.partial(pack_kernel, width),
        out_shape=jax.ShapeDtypeStruct((slots, width - 1, edge, 2 * T), F32),
        grid_spec=pltpu.PrefetchScalarGridSpec(
            num_scalar_prefetch=2,
            grid=(slots,),
            in_specs=[pl.BlockSpec((1,) + child.shape[1:], lambda s, o, e: (o[s], 0, 0))],
            out_specs=pl.BlockSpec((1, width - 1, edge, 2 * T), lambda s, o, e: (s, 0, 0, 0)),
        ),
        cost_estimate=pl.CostEstimate(
            flops=0, transcendentals=0, bytes_accessed=8 * slots * child.shape[1] * T
        ),
    )(order, spare, child)


def panel_kernel(mine_at, sib_at, use, own, mine, sib, out):
    row = pl.program_id(0)
    keep, use_mine, use_sib = use[0, row], use[1, row], use[2, row]
    value = jnp.where(keep > 0, own[0], 0.0)
    value = value + jnp.where(use_mine > 0, mine[0], 0.0)
    out[0] = value + jnp.where(use_sib > 0, sib[0], 0.0)


def panel_column(own, mine, sib, mine_at, sib_at, use):
    rows, edge, _ = own.shape
    block = (1, edge, edge)
    return pl.pallas_call(
        panel_kernel,
        out_shape=jax.ShapeDtypeStruct(own.shape, F32),
        grid_spec=pltpu.PrefetchScalarGridSpec(
            num_scalar_prefetch=3,
            grid=(rows,),
            in_specs=[
                pl.BlockSpec(block, lambda r, m, s, u: (r, 0, 0)),
                pl.BlockSpec(block, lambda r, m, s, u: (m[r], 0, 0)),
                pl.BlockSpec(block, lambda r, m, s, u: (s[r], 0, 0)),
            ],
            out_specs=pl.BlockSpec(block, lambda r, m, s, u: (r, 0, 0)),
        ),
        cost_estimate=pl.CostEstimate(
            flops=0, transcendentals=0, bytes_accessed=16 * rows * edge * edge
        ),
    )(mine_at, sib_at, use, own, mine, sib)


def eliminate(sym):
    lane = lax.broadcasted_iota(jnp.int32, (8, T), 1)
    sub = lax.broadcasted_iota(jnp.int32, (8, T), 0)
    count = T // 8
    wide = lambda x: jnp.broadcast_to(x, (8, T))
    a = [sym[8 * g : 8 * g + 8, :] for g in range(count)]
    w = [jnp.where(sub + 8 * g == lane, 1.0, 0.0).astype(F32) for g in range(count)]
    for k in range(0, T, STEP):
        g0, s0 = divmod(k, 8)
        rows = [wide(a[g0][s0 + j : s0 + j + 1, :]) for j in range(STEP)]
        wrows = [wide(w[g0][s0 + j : s0 + j + 1, :]) for j in range(STEP)]
        tiny = [[wide(rows[i][:, k + j : k + j + 1]) for j in range(STEP)] for i in range(STEP)]
        ratio = [[None] * STEP for _ in range(STEP)]
        roots, inverses = [], []
        for i in range(STEP):
            root = lax.rsqrt(tiny[i][i])
            inverse = root * root
            roots.append(root)
            inverses.append(inverse)
            for j in range(i + 1, STEP):
                ratio[j][i] = tiny[i][j] * inverse
            for j in range(i + 1, STEP):
                for m in range(j, STEP):
                    tiny[j][m] = tiny[j][m] - ratio[j][i] * tiny[i][m]
                rows[j] = rows[j] - ratio[j][i] * rows[i]
                wrows[j] = wrows[j] - ratio[j][i] * wrows[i]
        scaled = [rows[i] * inverses[i] for i in range(STEP)]
        wscaled = [wrows[i] * inverses[i] for i in range(STEP)]
        for g in range(g0, count):
            columns = [wide(a[g][:, k + j : k + j + 1]) for j in range(STEP)]
            for i in range(STEP):
                for j in range(i + 1, STEP):
                    columns[j] = columns[j] - columns[i] * ratio[j][i]
            next_a, next_w = a[g], w[g]
            for i in range(STEP):
                next_a = next_a - columns[i] * scaled[i]
                next_w = next_w - columns[i] * wscaled[i]
            if g == g0:
                later = sub >= s0 + STEP
                next_a = jnp.where(later, next_a, a[g])
                next_w = jnp.where(later, next_w, w[g])
                for i in range(STEP):
                    here = sub == s0 + i
                    next_a = jnp.where(here, rows[i] * roots[i], next_a)
                    next_w = jnp.where(here, wrows[i] * roots[i], next_w)
            a[g], w[g] = next_a, next_w
    return jnp.concatenate(a, axis=0), jnp.concatenate(w, axis=0)


def factor_steps(a, inv, start, stop, count):
    size = count * T
    row_id = lax.broadcasted_iota(jnp.int32, (T, T), 0)
    col_id = lax.broadcasted_iota(jnp.int32, (T, T), 1)
    full_row = lax.broadcasted_iota(jnp.int32, (size, T), 0)

    def step(kb, carry):
        at = pl.multiple_of(kb * T, T)
        block = a[pl.ds(at, T), pl.ds(at, T)]
        sym = jnp.where(row_id >= col_id, block, block.T)
        upper, inverse = eliminate(sym)
        inverse = jnp.where(row_id >= col_id, inverse, 0.0)
        lower = jnp.where(col_id >= row_id, upper, 0.0).T
        inv[kb] = inverse
        strip = a[:, pl.ds(at, T)]
        below = jnp.where(full_row >= at + T, dot6(strip, inverse, NT), 0.0)
        a[:, pl.ds(at, T)] = jnp.where(full_row >= at + T, below, strip)
        a[pl.ds(at, T), pl.ds(at, T)] = lower

        def update(i, c):
            top = pl.multiple_of(i * T, T)
            rows = a[pl.ds(top, T), pl.ds(at, T)]
            a[pl.ds(top, T), :] = a[pl.ds(top, T), :] - dot6(rows, below, NT)
            return c

        return lax.fori_loop(kb + 1, count, update, carry)

    lax.fori_loop(start, stop, step, 0)


def factor_first(stop, here, even, odd, a, inv):
    edge = even.shape[2]
    row, col, cols = here[0], here[1], here[2]
    for i in range(NB):
        at = i ^ row
        for j in range(NB):
            spot = (slice(i * edge, i * edge + edge), slice(j * edge, j * edge + edge))
            if j <= i:
                turn = lax.rem(col - j + cols, cols)
                same, other = even[turn, at // 2], odd[turn, at // 2]
                a[spot] = jnp.where(at % 2 == 0, same, other)
            else:
                a[spot] = jnp.zeros((edge, edge), F32)
    factor_steps(a, inv, 0, stop, a.shape[0] // T)


def factor_second(start, a_in, inv_in, l_out, lh_out, ll_out, wh_out, wl_out, a, inv):
    count = a.shape[0] // T
    edge = wh_out.shape[1]
    per = edge // T
    for i in range(count):
        rows = slice(i * T, i * T + T)
        a[rows, :] = a_in[rows, :]
    for i in range(start):
        inv[i] = inv_in[i]
    factor_steps(a, inv, start, count, count)
    for i in range(count):
        rows = slice(i * T, i * T + T)
        for j in range(i + 1, count):
            a[rows, j * T : j * T + T] = jnp.zeros((T, T), F32)
        value = a[rows, :]
        l_out[rows, :] = value
        high, low = split(value)
        lh_out[rows, :] = high
        ll_out[rows, :] = low
    for b in range(NB):
        for i in range(per):
            for j in range(per):
                spot = (b, slice(i * T, i * T + T), slice(j * T, j * T + T))
                if i == j:
                    value = inv[b * per + i]
                elif i < j:
                    value = jnp.zeros((T, T), F32)
                else:
                    top, left = (b * per + i) * T, (b * per + j) * T
                    under = a[top : top + T, left : left + T]
                    value = -dot6(inv[b * per + i], dot6(under, inv[b * per + j], NN), NN)
                high, low = split(value)
                wh_out[spot] = high
                wl_out[spot] = low


VMEM_SPEC = pl.BlockSpec(memory_space=pltpu.VMEM)


def factor_start(even, odd, here):
    edge = even.shape[2]
    size = NB * edge
    assert edge == 2 * T
    return pl.pallas_call(
        functools.partial(factor_first, size // (2 * T)),
        out_shape=(
            jax.ShapeDtypeStruct((size, size), F32),
            jax.ShapeDtypeStruct((size // T, T, T), F32),
        ),
        in_specs=[pl.BlockSpec(memory_space=pltpu.SMEM), VMEM_SPEC, VMEM_SPEC],
        out_specs=(VMEM_SPEC,) * 2,
        compiler_params=pltpu.CompilerParams(vmem_limit_bytes=40 * MIB),
        cost_estimate=pl.CostEstimate(
            flops=60_000_000_000, transcendentals=0, bytes_accessed=8 * size * size
        ),
    )(here, even, odd)


def factor_end(a, inv, edge):
    size = a.shape[0]
    return pl.pallas_call(
        functools.partial(factor_second, size // (2 * T)),
        out_shape=(
            jax.ShapeDtypeStruct((size, size), F32),
            jax.ShapeDtypeStruct((size, size), BF16),
            jax.ShapeDtypeStruct((size, size), BF16),
            jax.ShapeDtypeStruct((NB, edge, edge), BF16),
            jax.ShapeDtypeStruct((NB, edge, edge), BF16),
        ),
        in_specs=[VMEM_SPEC] * 2,
        out_specs=(VMEM_SPEC,) * 5,
        scratch_shapes=[pltpu.VMEM((size, size), F32), pltpu.VMEM((size // T, T, T), F32)],
        compiler_params=pltpu.CompilerParams(vmem_limit_bytes=40 * MIB),
        cost_estimate=pl.CostEstimate(
            flops=60_000_000_000, transcendentals=0, bytes_accessed=16 * size * size
        ),
    )(a, inv)


def substitute(pieces, lh, ll, wh, wl):
    edge = wh.shape[1]
    solved = []
    for j in range(NB):
        value = pieces[j]
        for k in range(j):
            spot = (slice(j * edge, j * edge + edge), slice(k * edge, k * edge + edge))
            value = value - dot3(*solved[k][:2], lh[spot], ll[spot])
        value = dot3(*split(value), wh[j], wl[j])
        solved.append(split(value) + (value,))
    return solved


def solve_rows_kernel(words, *refs):
    count = len(refs) - 7
    raw = refs[:count]
    lh, ll, wh, wl, high_out, low_out, own_out = refs[count:]
    edge = wh.shape[1]
    at = pl.program_id(0)
    col = words[NB, 0]
    pieces = []
    for j in range(NB):
        turn = j - col + count // 2
        value = raw[0][0]
        for step in range(1, count):
            value = jnp.where(turn == step, raw[step][0], value)
        pieces.append(value)
    own = None
    for j, (high, low, value) in enumerate(substitute(pieces, lh, ll, wh, wl)):
        used = words[j, at] > 0
        spot = slice(j * edge, j * edge + edge)
        zero = jnp.zeros_like(high)
        high_out[:, spot] = jnp.where(used, high, zero)
        low_out[:, spot] = jnp.where(used, low, zero)
        mine = jnp.where(col == j, value, 0.0)
        own = mine if own is None else own + mine
    own_out[...] = own


def solve_cols_kernel(count, words, *refs):
    raw = refs[:count]
    lh, ll, wh, wl = refs[count : count + 4]
    high_out, low_out = refs[-2:]
    edge = wh.shape[1]
    source = pl.program_id(0)
    share = source ^ words[0]
    pieces = []
    for j in range(NB):
        turn = lax.rem(share - j + count, count)
        value = raw[0][turn]
        for at in range(1, count):
            value = jnp.where(source == at, raw[at][turn], value)
        pieces.append(value)
    for j, (high, low, _) in enumerate(substitute(pieces, lh, ll, wh, wl)):
        spot = slice(j * edge, j * edge + edge)
        high_out[:, spot] = high
        low_out[:, spot] = low


def solve_cost(rows, edge):
    return pl.CostEstimate(
        flops=60 * rows * edge * edge, transcendentals=0, bytes_accessed=32 * rows * edge
    )


def solve_rows(raw, words, factor):
    groups, edge, _ = raw[0].shape
    size = NB * edge
    whole = lambda array: pl.BlockSpec(array.shape, lambda g, k: (0,) * array.ndim)
    return pl.pallas_call(
        solve_rows_kernel,
        out_shape=(
            jax.ShapeDtypeStruct((groups * edge, size), BF16),
            jax.ShapeDtypeStruct((groups * edge, size), BF16),
            jax.ShapeDtypeStruct((groups * edge, edge), F32),
        ),
        grid_spec=pltpu.PrefetchScalarGridSpec(
            num_scalar_prefetch=1,
            grid=(groups,),
            in_specs=[pl.BlockSpec((1, edge, edge), lambda g, k: (g, 0, 0))] * len(raw)
            + [whole(x) for x in factor[1:]],
            out_specs=(
                pl.BlockSpec((edge, size), lambda g, k: (g, 0)),
                pl.BlockSpec((edge, size), lambda g, k: (g, 0)),
                pl.BlockSpec((edge, edge), lambda g, k: (g, 0)),
            ),
        ),
        compiler_params=pltpu.CompilerParams(vmem_limit_bytes=40 * MIB),
        cost_estimate=solve_cost(groups * edge, edge),
    )(words, *raw, *factor[1:])


def solve_cols(raw, factor, words, leafs, before=()):
    count = len(raw)
    _, rows, edge = raw[0].shape
    size = NB * edge
    vmem = pl.BlockSpec(memory_space=pltpu.VMEM)
    return pl.pallas_call(
        functools.partial(solve_cols_kernel, count),
        out_shape=(jax.ShapeDtypeStruct((leafs * count * rows, size), BF16),) * 2,
        grid_spec=pltpu.PrefetchScalarGridSpec(
            num_scalar_prefetch=1,
            grid=(count,),
            in_specs=[vmem] * (count + 4) + [pl.BlockSpec(memory_space=pl.ANY)] * len(before),
            out_specs=(
                pl.BlockSpec((rows, size), lambda i, w: (w[1] * count + (i ^ w[0]), 0)),
            )
            * 2,
        ),
        input_output_aliases={count + 5 + at: at for at in range(len(before))},
        compiler_params=pltpu.CompilerParams(vmem_limit_bytes=48 * MIB),
        cost_estimate=solve_cost(count * rows, edge),
    )(words, *raw, *factor[1:], *before)


def extend_kernel(cols, child_cols, rowtab, coltab, keep, own, mine, out):
    row = pl.program_id(0)
    edge = out.shape[2]
    has_mine = rowtab[2, row]

    def one(j, carry):
        at_mine = coltab[0, j]
        add_mine = (at_mine >= 0) & (has_mine > 0)
        from_mine = jnp.maximum(at_mine, 0)
        for half in range(2):
            lanes = slice(half * T, half * T + T)
            spot = pl.ds(2 * j + half, edge, stride=2 * cols)
            value = jnp.where(keep[row, j] > 0, own[0, spot, :], 0.0)
            theirs = mine[0, pl.ds(2 * from_mine + half, edge, stride=2 * child_cols), :]
            out[0, j, :, lanes] = value + jnp.where(add_mine, theirs, 0.0)
        return carry

    lax.fori_loop(0, cols, one, 0, unroll=2)


def extend(own, mine, rowtab, coltab, keep, edge):
    rows = own.shape[0]
    cols, child_cols = own.shape[1] // (2 * edge), mine.shape[1] // (2 * edge)
    return pl.pallas_call(
        functools.partial(extend_kernel, cols, child_cols),
        out_shape=jax.ShapeDtypeStruct((rows, cols, edge, edge), F32),
        grid_spec=pltpu.PrefetchScalarGridSpec(
            num_scalar_prefetch=3,
            grid=(rows,),
            in_specs=[
                pl.BlockSpec((1,) + own.shape[1:], lambda r, rt, *t: (r, 0, 0)),
                pl.BlockSpec((1,) + mine.shape[1:], lambda r, rt, *t: (rt[0, r], 0, 0)),
            ],
            out_specs=pl.BlockSpec((1, cols, edge, edge), lambda r, *t: (r, 0, 0, 0)),
        ),
        compiler_params=pltpu.CompilerParams(vmem_limit_bytes=40 * MIB),
        cost_estimate=pl.CostEstimate(
            flops=0, transcendentals=0, bytes_accessed=10 * rows * cols * edge * edge
        ),
    )(rowtab, coltab, keep, own, mine)


def finish_kernel(
    cols, leafs, early, base, rowtab, coltab,
    blocks, sib, late, rest, sib_e, panel, srh, srl, sch, scl, out,
):
    row = pl.program_id(0)
    edge = srh.shape[0]
    has_sib, slot = rowtab[3, row], rowtab[4, row]

    def one(j, carry):
        total = dot3(srh[...], srl[...], sch[j % leafs, j // leafs], scl[j % leafs, j // leafs])
        at_sib = coltab[1, j]
        add_sib = (at_sib >= 0) & (has_sib > 0)
        at_sib = jnp.maximum(at_sib, 0)
        for half in range(2):
            lanes = slice(half * T, half * T + T)
            theirs = jnp.where(slot < base, late[0, at_sib, :, lanes], rest[0, at_sib, :, lanes])
            theirs = jnp.where(slot < early, sib[0, at_sib, :, lanes], theirs)
            value = blocks[0, j, :, lanes] + jnp.where(add_sib, theirs, 0.0)
            out[0, pl.ds(2 * j + half, edge, stride=2 * cols), :] = value - total[:, lanes]
        return carry

    lax.fori_loop(0, cols, one, 0, unroll=8)
    extra = coltab[2, 0]

    @pl.when((extra >= 0) & (has_sib > 0))
    def _():
        for half in range(2):
            spot = pl.ds(2 * jnp.maximum(extra, 0) + half, edge, stride=2 * cols)
            out[0, spot, :] = out[0, spot, :] + sib_e[0, :, half * T : half * T + T]

    @pl.when(coltab[2, 1] > 0)
    def _():
        for half in range(2):
            spot = pl.ds(half, edge, stride=2 * cols)
            out[0, spot, :] = panel[0, :, half * T : half * T + T]


def finish(blocks, sib, late, rest, sib_e, panel, s_row, s_col, rowtab, coltab, leafs):
    rows, cols, edge, _ = blocks.shape
    size = s_row[0].shape[1]
    early = sib.shape[0]
    base = early + late.shape[0]
    s_col = [s.reshape(leafs, rows, edge, size) for s in s_col]
    column_spec = pl.BlockSpec(
        s_col[0].shape, lambda r, *t: (0, 0, 0, 0), pipeline_mode=pl.Buffered(1)
    )
    row_spec = pl.BlockSpec((edge, size), lambda r, *t: (r, 0))
    piece = (1,) + sib.shape[1:]
    lines = 2 * cols * edge
    return pl.pallas_call(
        functools.partial(finish_kernel, cols, leafs, early, base),
        out_shape=jax.ShapeDtypeStruct((rows, lines, T), F32),
        grid_spec=pltpu.PrefetchScalarGridSpec(
            num_scalar_prefetch=2,
            grid=(rows,),
            in_specs=[
                pl.BlockSpec((1, cols, edge, edge), lambda r, *t: (r, 0, 0, 0)),
                pl.BlockSpec(piece, lambda r, rt, *t: (jnp.minimum(rt[4, r], early - 1), 0, 0, 0)),
                pl.BlockSpec(
                    piece, lambda r, rt, *t: (jnp.clip(rt[4, r] - early, 0, base - early - 1), 0, 0, 0)
                ),
                pl.BlockSpec(piece, lambda r, rt, *t: (jnp.maximum(rt[4, r] - base, 0), 0, 0, 0)),
                pl.BlockSpec((1, edge, edge), lambda r, rt, *t: (rt[1, r], 0, 0)),
                pl.BlockSpec((1, edge, edge), lambda r, rt, *t: (r, 0, 0)),
                row_spec,
                row_spec,
                column_spec,
                column_spec,
            ],
            out_specs=pl.BlockSpec((1, lines, T), lambda r, *t: (r, 0, 0)),
        ),
        compiler_params=pltpu.CompilerParams(vmem_limit_bytes=58 * MIB),
        cost_estimate=pl.CostEstimate(
            flops=6 * rows * cols * edge * edge * size,
            transcendentals=0,
            bytes_accessed=12 * rows * cols * edge * edge,
        ),
    )(rowtab, coltab, blocks, sib, late, rest, sib_e, panel, *s_row, *s_col)


def pick(table, size):
    want = jnp.arange(size, dtype=jnp.int32)
    same = table[..., None, :] == want[:, None]
    place = jnp.arange(table.shape[-1], dtype=jnp.int32)
    return jnp.sum(jnp.where(same, place, 0), axis=-1), jnp.any(same, axis=-1)


def pairs(count, distance):
    return [(i, i ^ distance) for i in range(count)]


def turns(count):
    return [[(i, (i + step) % count) for i in range(count)] for step in range(1, count)]


def shards(parent_entries, block_pattern, child_map, child_schur):
    leafs = lax.axis_size("leaf")
    row_count = lax.axis_size("row")
    grid_rows = leafs * row_count
    grid_cols = lax.axis_size("col")
    leaf = lax.axis_index("leaf")
    row = lax.axis_index("row")
    col = lax.axis_index("col")
    here_rows = leaf * row_count + row
    local_rows, _, edge, local_cols, _, _ = parent_entries.shape
    _, child_rows, _, _, child_cols, _, _ = child_schur.shape
    assert leafs == 2 and row_count == grid_cols and NB <= grid_cols
    own = parent_entries.reshape(local_rows, edge * local_cols * edge // T, T)
    child = child_schur.reshape(child_rows, edge * child_cols * edge // T, T)

    grid = child_map.reshape(leafs, -1, grid_cols)
    ids = jnp.arange(grid_cols, dtype=jnp.int32)
    row_levels = jnp.sum(jnp.where(ids == row, grid, 0), axis=2) // grid_cols
    col_levels = jnp.sum(jnp.where(ids == col, grid, 0), axis=2) // grid_cols
    row_levels = jnp.where(leaf == 0, row_levels, row_levels[::-1])
    col_levels = jnp.where(leaf == 0, col_levels, col_levels[::-1])
    owner = jnp.stack([leaf, 1 - leaf])[:, None]
    moves = (row_levels % leafs != owner).astype(jnp.int32)
    before = jnp.arange(child_rows)[:, None] > jnp.arange(child_rows)[None, :]
    moved = jnp.sum(jnp.where(before, moves[:, None, :], 0), axis=2)
    stayed = jnp.arange(child_rows) - moved + jnp.sum(moves, axis=1, keepdims=True)
    slot = jnp.where(moves > 0, moved, stayed)
    order, _ = pick(slot[0], child_rows)
    local = jnp.where(row_levels % leafs == leaf, row_levels // leafs, -1)
    at_row, has_row = pick(local, local_rows)
    at_slot = jnp.sum(
        jnp.where(at_row[1][:, None] == jnp.arange(child_rows), slot[1][None, :], 0), axis=1
    )
    at_slot = jnp.where(has_row[1], at_slot, 0)
    at_col, has_col = pick(col_levels, local_cols)
    spare = at_col[:, 0]
    is_spare = has_col[1] & (at_col[1] == spare[1])
    columns = jnp.arange(local_cols, dtype=jnp.int32)
    extra = jnp.sum(jnp.where(is_spare, columns + 1, 0)) - 1
    block_rows = jnp.arange(local_rows, dtype=jnp.int32) * grid_rows + here_rows
    block_cols = columns * grid_cols + col
    pattern = block_pattern.reshape(local_rows, grid_rows, local_cols, grid_cols)
    mine_here = (jnp.arange(grid_rows) == here_rows)[:, None, None] & (ids == col)
    keep = jnp.sum(jnp.where(mine_here, pattern, 0), axis=(1, 3))
    keep = jnp.maximum(keep, (block_rows[:, None] == block_cols[None, :]).astype(jnp.int32))
    keep = keep.astype(jnp.int32)
    is_panel = (col < NB).astype(jnp.int32)
    row_use = has_row.astype(jnp.int32)
    rowtab = jnp.concatenate([at_row, row_use, at_slot[None]], axis=0).astype(jnp.int32)
    packed = at_col[1] - (at_col[1] > spare[1])
    tail = jnp.where(columns == 0, extra, jnp.where(columns == 1, is_panel, 0))
    coltab = jnp.stack(
        [jnp.where(has_col[0], at_col[0], -1), jnp.where(has_col[1] & ~is_spare, packed, -1), tail]
    ).astype(jnp.int32)
    col_use = has_col[:, 0].astype(jnp.int32)
    use = jnp.stack([keep[:, 0], row_use[0] * col_use[0], row_use[1] * col_use[1]])

    swap = [(i, i ^ 1) for i in range(leafs)]
    mine_e = lax.dynamic_index_in_dim(child_schur[0, :, 0, :, :, 0, :], spare[0], 2, keepdims=False)
    lead, has_lead = pick(row_levels[0], 1)
    block = jnp.where(
        has_lead[0] & has_col[0, 0],
        lax.dynamic_index_in_dim(mine_e, lead[0], 0, keepdims=False),
        0.0,
    )
    block = block + jnp.where(
        (leaf == 0) & (keep[0, 0] > 0), parent_entries[0, 0, :, 0, 0, :], 0.0
    )
    come = lax.ppermute(block, "leaf", swap)
    come, mine_e = lax.optimization_barrier((come, mine_e))
    sib_e = lax.ppermute(mine_e, "leaf", swap)
    base = -(-3 * child_rows // 4)
    early = max(base // 3, 1)
    bulk = pack(child, order, spare[:1], early, child_cols)
    bulk_late = pack(child, order[early:], spare[:1], base - early, child_cols)
    bulk, bulk_late, come = lax.optimization_barrier((bulk, bulk_late, come))
    block = (block + come)[None]
    distance = 2
    while distance < row_count:
        other = lax.ppermute(block, "row", pairs(row_count, distance))
        block = jnp.concatenate([block, other], axis=0)
        distance *= 2
    line = [block] + [lax.ppermute(block, "col", turn) for turn in turns(grid_cols)]
    even = jnp.stack(line, axis=0)
    odd = lax.ppermute(even, "row", pairs(row_count, 1))

    bulk, sib_e = lax.optimization_barrier((bulk, sib_e))
    sib = lax.ppermute(bulk, "leaf", swap)
    sib_late = lax.ppermute(bulk_late, "leaf", swap)
    column = panel_column(
        parent_entries[:, 0, :, 0, 0, :], mine_e, sib_e, at_row[0], at_row[1], use
    )
    even, column = lax.optimization_barrier((even, column))

    share = local_rows * edge // row_count
    pieces = column.reshape(row_count, share, edge)
    got = []
    for step in range(row_count):
        send = lax.dynamic_index_in_dim(pieces, (col + step) % row_count, 0, keepdims=False)
        route = [
            (r * grid_cols + c, ((c + step) % row_count) * grid_cols + r)
            for r in range(row_count)
            for c in range(grid_cols)
        ]
        got.append(lax.ppermute(send, ("row", "col"), route))
    up = [(i, i + 1) for i in range(grid_cols - 1)]
    down = [(i + 1, i) for i in range(grid_cols - 1)]
    line = [column]

    def onward(low, high):
        low, high = lax.ppermute(low, "col", up), lax.ppermute(high, "col", down)
        line.insert(0, low)
        line.append(high)
        return low, high

    words = jnp.stack([row, col, jnp.int32(grid_cols)])
    state = factor_start(even, odd, words)
    got, state, column = lax.optimization_barrier((got, state, column))
    line[0] = column
    ends = onward(column, column)
    got = jnp.stack(got, axis=0)
    theirs = lax.ppermute(got, "leaf", swap)

    def over_rows(part):
        parts = [part]
        distance = 2
        while distance < row_count:
            parts += [lax.ppermute(x, "row", pairs(row_count, distance)) for x in parts]
            distance *= 2
        return parts

    def over_cores(parts):
        across = [lax.ppermute(x, "row", pairs(row_count, 1)) for x in parts]
        return [x for two in zip(parts, across) for x in two]

    ours = over_rows(got)
    factor = factor_end(*state, edge)
    factor, ends, rowtab = lax.optimization_barrier((factor, ends, rowtab))
    line[0], line[-1] = ends
    if grid_cols > 2:
        ends = onward(*ends)
    blocks = extend(own, child, rowtab, coltab, keep, edge)
    blocks, ends, theirs, ours = lax.optimization_barrier((blocks, ends, theirs, ours))
    line[0], line[-1] = ends
    for _ in range(3, grid_cols):
        ends = onward(*ends)
    theirs = over_rows(theirs)
    s_col = solve_cols(over_cores(ours), factor, jnp.stack([row, leaf]), leafs)
    ends, theirs, s_col = lax.optimization_barrier((ends, theirs, s_col))
    line[0], line[-1] = ends
    theirs = over_cores(theirs)
    row_keep = block_rows[None, :] >= PB * (jnp.arange(NB, dtype=jnp.int32)[:, None] // PB + 1)
    col_word = jnp.broadcast_to(col, (1, local_rows))
    row_keep = jnp.concatenate([row_keep.astype(jnp.int32), col_word], axis=0)
    srh, srl, solved = solve_rows(line, row_keep, factor)
    s_col = solve_cols(theirs, factor, jnp.stack([row, 1 - leaf]), leafs, s_col)

    solved = solved.reshape(local_rows, edge, edge)
    at = jnp.minimum(here_rows, NB - 1) * edge, jnp.minimum(col, NB - 1) * edge
    piece = lax.dynamic_slice(factor[0], at, (edge, edge))
    first = jnp.where(
        (here_rows // PB) > col // PB,
        solved[0],
        jnp.where(here_rows // PB == col // PB, piece, column[0]),
    )
    panel = solved.at[0].set(first)

    def fetch():
        more = pack(child, order[base:], spare[:1], child_rows - base, child_cols)
        return lax.ppermute(more, "leaf", swap)

    def nothing():
        return jnp.zeros((child_rows - base, child_cols - 1, edge, edge), F32)

    levels = child_map.reshape(leafs, -1, grid_cols) // grid_cols
    crossing = levels % leafs != jnp.arange(leafs)[:, None, None]
    most = jnp.max(jnp.sum(crossing.astype(jnp.int32), axis=1))
    rest = lax.cond(most > base, fetch, nothing)
    out = finish(blocks, sib, sib_late, rest, sib_e, panel, (srh, srl), s_col, rowtab, coltab, leafs)
    return out.reshape(parent_entries.shape)


def solution(mesh):
    return jax.shard_map(
        shards,
        mesh=mesh,
        in_specs=(
            P(None, ("leaf", "row"), None, None, "col", None),
            P(),
            P(),
            P("leaf", None, "row", None, None, "col", None),
        ),
        out_specs=P(None, ("leaf", "row"), None, None, "col", None),
        check_vma=False,
    )
```
